32 devices in a mesh: rep: 8 (over y, x, core), fsdp: 4 (over z).
Axes of the slice: x: 2, y: 2, z: 4, core: 2. Of those that a mesh axis runs over, the one named last changes fastest.
Arguments:
- tokens: bfloat16 [8, 2048, 1088], P('rep', 'fsdp'), may hold values from -6 to 6
- w_qkv: bfloat16 [1088, 3264], P('fsdp'), may hold values from -0.1875 to 0.1875
- qv_bias: bfloat16 [2176], P('fsdp'), may hold values from -0.29882812 to 0.29882812
- w_out: bfloat16 [1088, 1088], P('fsdp'), may hold values from -1.5 to 1.5
- out_bias: bfloat16 [1088], P('fsdp'), may hold values from -1.796875 to 1.796875
- w_up: bfloat16 [1088, 4352], P('fsdp'), may hold values from -0.1875 to 0.1875
- up_bias: bfloat16 [4352], P('fsdp'), may hold values from -3 to 3
- w_down: bfloat16 [4352, 1088], P('fsdp'), may hold values from -0.09375 to 0.09375
- down_bias: bfloat16 [1088], P('fsdp'), may hold values from -1.796875 to 1.796875
- ln1_gain: bfloat16 [1088], P('fsdp'), may hold values from 0.099609375 to 1.8984375
- ln1_bias: bfloat16 [1088], P('fsdp'), may hold values from -3 to 3
- ln2_gain: bfloat16 [1088], P('fsdp'), may hold values from 0.099609375 to 1.8984375
- ln2_bias: bfloat16 [1088], P('fsdp'), may hold values from -3 to 3
- cotangent: bfloat16 [8, 2048, 1088], P('rep', 'fsdp'), may hold values from -6 to 6
Outputs:
- layer_out: float32 [8, 2048, 1088], P('rep', 'fsdp')
- grad_tokens: float32 [8, 2048, 1088], P('rep', 'fsdp')
- grad_w_qkv: float32 [1088, 3264], P('fsdp')
- grad_qv_bias: float32 [2176], P('fsdp')
- grad_w_out: float32 [1088, 1088], P('fsdp')
- grad_out_bias: float32 [1088], P('fsdp')
- grad_w_up: float32 [1088, 4352], P('fsdp')
- grad_up_bias: float32 [4352], P('fsdp')
- grad_w_down: float32 [4352, 1088], P('fsdp')
- grad_down_bias: float32 [1088], P('fsdp')
- grad_ln1_gain: float32 [1088], P('fsdp')
- grad_ln1_bias: float32 [1088], P('fsdp')
- grad_ln2_gain: float32 [1088], P('fsdp')
- grad_ln2_bias: float32 [1088], P('fsdp')
The draws below stay inside these ranges and needn't reach their ends.
All inputs are finite; a program needn't handle non-finite values.
Results may differ from the reference program's by a relative error of at most 0.012.
Values may be sent and summed in bfloat16 or wider, within the bound.
No kernel may reach another device: no remote copies, remote signals or barrier semaphores. Data moves between devices by JAX's collectives and lax.ppermute only.
A program may use at most 256 MiB of HBM per device.

```python
import jax
import jax.numpy as jnp
from jax import lax

D = 1088
HEADS = 17
HD = 64
FF = 4352
LEN = 2048
SEQS = 8


def block_scale(key, extent, pieces, smallest, largest):
    loudness = 1.0
    for axis_at, blocks in pieces:
        draws = jax.random.uniform(jax.random.fold_in(jax.random.fold_in(key, 6), axis_at), (blocks,), jnp.float32, smallest / len(pieces), largest / len(pieces))
        loudness = loudness * jnp.repeat(jnp.exp(draws), extent[axis_at] // blocks).reshape((-1,) + (1,) * (len(extent) - 1 - axis_at))
    return loudness


def centred(own_key, shape, scale, limit, pieces=(), held_as=jnp.bfloat16):
    level = block_scale(own_key, shape, pieces, -0.22, 0.18) if pieces else 1.0
    values = jax.random.normal(own_key, shape, jnp.float32) * scale * level
    return jnp.minimum(jnp.maximum(values, -limit), limit).astype(held_as)


def setup_inputs(seed: int = 0) -> dict:
    key_of = jax.random.split(jax.random.key(seed), 15)
    return {
        "tokens": centred(key_of[0], (SEQS, LEN, D), 1.0, 6.0, ((0, 8), (1, 4))),
        "w_qkv": centred(key_of[1], (D, 3 * D), D ** -0.5, 0.1875, ((0, 4),)),
        "qv_bias": centred(key_of[2], (2 * D,), 0.05, 0.29882812, ((0, 4),)),
        "w_out": centred(key_of[3], (D, D), (D // 64) ** -0.5, 1.5, ((0, 4),)),
        "out_bias": centred(key_of[4], (D,), 0.3, 1.796875, ((0, 4),)),
        "w_up": centred(key_of[5], (D, FF), D ** -0.5, 0.1875, ((0, 4),)),
        "up_bias": centred(key_of[6], (FF,), 0.5, 3.0, ((0, 4),)),
        "w_down": centred(key_of[7], (FF, D), FF ** -0.5, 0.09375, ((0, 4),)),
        "down_bias": centred(key_of[8], (D,), 0.3, 1.796875, ((0, 4),)),
        "ln1_gain": jnp.clip(1.0 + 0.18 * jax.random.normal(key_of[9], (D,), jnp.float32), 0.099609375, 1.8984375).astype(jnp.bfloat16),
        "ln1_bias": centred(key_of[10], (D,), 0.5, 3.0, ((0, 4),)),
        "ln2_gain": jnp.clip(1.0 + 0.18 * jax.random.normal(key_of[11], (D,), jnp.float32), 0.099609375, 1.8984375).astype(jnp.bfloat16),
        "ln2_bias": centred(key_of[12], (D,), 0.5, 3.0, ((0, 4),)),
        "cotangent": centred(key_of[13], (SEQS, LEN, D), 1.0, 6.0, ((0, 8), (1, 4))),
    }


HIGH = lax.Precision.HIGHEST
EPSILON = 1e-05

@jax.custom_vjp
def low(v):
    return lax.optimization_barrier(v.astype(jnp.bfloat16)).astype(jnp.float32)

@jax.custom_vjp
def low_back(v):
    return v

def low_keep(v):
    return (low(v), None)

def low_pass(kept, grad):
    return (grad,)

def back_keep(v):
    return (v, None)

def back_low(kept, grad):
    return (low(grad),)
low.defvjp(low_keep, low_pass)
low_back.defvjp(back_keep, back_low)

def normalize(vector):
    centre = vector - lax.optimization_barrier(jnp.mean(vector, axis=-1, keepdims=True))
    inverse = lax.rsqrt(lax.optimization_barrier(jnp.mean(centre * centre, axis=-1, keepdims=True)) + EPSILON)
    return centre * inverse

def gelu_exact(vector):
    return jax.nn.gelu(vector, approximate=False)

def matmul(left_side, right_side):
    return jnp.dot(left_side, right_side, precision=HIGH, preferred_element_type=jnp.float32)

def attend(queries, keys, values):
    block_rows = min(512, LEN)
    block_count = LEN // block_rows
    positions = jnp.arange(LEN, dtype=jnp.int32)
    scale = HD ** (-0.5)

    def one_block(block_index):
        start = block_index.astype(jnp.int32) * block_rows
        query_part = lax.dynamic_slice_in_dim(queries, start, block_rows, 0)
        scores = jnp.einsum('qhd,khd->hqk', query_part, keys, precision=HIGH) * scale
        scores = low_back(scores)
        query_pos = start + jnp.arange(block_rows, dtype=jnp.int32)
        allowed = positions[None, :] <= query_pos[:, None]
        scores = jnp.where(allowed[None], scores, -1e+30)
        row_peak = lax.optimization_barrier(jnp.max(scores, axis=-1, keepdims=True))
        weights = jnp.exp(scores - row_peak)
        probabilities = weights / lax.optimization_barrier(jnp.sum(weights, axis=-1, keepdims=True))
        return jnp.einsum('hqk,khd->qhd', low(probabilities), values, precision=HIGH)
    blocks = lax.map(jax.checkpoint(one_block), jnp.arange(block_count, dtype=jnp.int32))
    return blocks.reshape(LEN, HEADS * HD)

def layer(sequence, params):
    w_qkv, qv_bias, w_out, out_bias, w_up, up_bias, w_down, down_bias, ln1_gain, ln1_bias, ln2_gain, ln2_bias = params
    first = low(normalize(sequence) * ln1_gain + ln1_bias)
    zero_keys = jnp.zeros((D,), jnp.float32)
    full_bias = jnp.concatenate([qv_bias[:D], zero_keys, qv_bias[D:]])
    mixed = low(low_back(matmul(first, w_qkv) + full_bias))
    queries = mixed[:, :D].reshape(LEN, HEADS, HD)
    keys = mixed[:, D:2 * D].reshape(LEN, HEADS, HD)
    values = mixed[:, 2 * D:].reshape(LEN, HEADS, HD)
    attended = low(low_back(attend(queries, keys, values)))
    branch = low_back(matmul(attended, w_out) + out_bias)
    hidden = sequence + branch
    second = low(normalize(hidden) * ln2_gain + ln2_bias)
    upward = low_back(matmul(second, w_up) + up_bias)
    activated = low(gelu_exact(upward))
    downward = low_back(matmul(activated, w_down) + down_bias)
    return hidden + downward

def reference(tokens, w_qkv, qv_bias, w_out, out_bias, w_up, up_bias, w_down, down_bias, ln1_gain, ln1_bias, ln2_gain, ln2_bias, cotangent):
    params = tuple((weight.astype(jnp.float32) for weight in (w_qkv, qv_bias, w_out, out_bias, w_up, up_bias, w_down, down_bias, ln1_gain, ln1_bias, ln2_gain, ln2_bias)))

    def one_sequence(running, inputs_pair):
        sequence, seq_grad = inputs_pair
        layer_result, pullback = jax.vjp(layer, sequence.astype(jnp.float32), params)
        input_grad, param_grads = pullback(seq_grad.astype(jnp.float32))
        running = jax.tree.map(lambda first_sum, second_sum: first_sum + second_sum, running, param_grads)
        return (running, (layer_result, input_grad))
    start_sums = tuple((jnp.zeros_like(weight) for weight in params))
    totals, (results, input_grads) = lax.scan(one_sequence, start_sums, (tokens, cotangent))
    return (results, input_grads, totals[0], totals[1], totals[2], totals[3], totals[4], totals[5], totals[6], totals[7], totals[8], totals[9], totals[10], totals[11])
```

```python
import jax
import jax.numpy as jnp
from jax import lax
from jax.sharding import PartitionSpec as P

HD = 64


EPSILON = 1e-05


def normalize(vector):
    centre = vector - jnp.mean(vector, axis=-1, keepdims=True)
    inverse = lax.rsqrt(jnp.mean(centre * centre, axis=-1, keepdims=True) + EPSILON)
    return centre * inverse


def gelu_exact(vector):
    return jax.nn.gelu(vector, approximate=False)


def local(
    tokens,
    w_qkv,
    qv_bias,
    w_out,
    out_bias,
    w_up,
    up_bias,
    w_down,
    down_bias,
    ln1_gain,
    ln1_bias,
    ln2_gain,
    ln2_bias,
    cotangent,
):
    seq_count, local_len, features = tokens.shape
    rows = w_qkv.shape[0]
    reps = lax.axis_size("rep")
    rep_at = lax.axis_index("rep")
    everyone = ("fsdp", "rep")

    def own_piece(matrix):
        part = matrix.shape[0] // reps
        return lax.dynamic_slice_in_dim(matrix, rep_at * part, part, 0)

    def to_units(matrix):
        blocks = matrix.shape[1] // features
        return matrix.reshape(rows, blocks, features).transpose(1, 0, 2)

    def gather_all(matrix):
        return lax.all_gather(own_piece(matrix), everyone, axis=0, tiled=True)

    def from_units(units):
        blocks = units.shape[1]
        return units.transpose(0, 2, 1, 3).reshape(features, blocks * features)

    pack_one = jnp.concatenate([to_units(w_qkv), to_units(w_out)], 0)
    units_one = gather_all(pack_one.reshape(-1, features)).reshape(-1, 4, rows, features)
    units_up = gather_all(to_units(w_up).reshape(-1, features)).reshape(-1, 4, rows, features)
    down_full = gather_all(w_down)
    qkv_full = from_units(units_one[:, :3])
    out_full = from_units(units_one[:, 3:])
    up_full = from_units(units_up)
    vectors = (qv_bias, out_bias, up_bias, down_bias, ln1_gain, ln1_bias, ln2_gain, ln2_bias)
    small = lax.all_gather(jnp.concatenate(vectors), "fsdp", axis=0)
    pieces = []
    start = 0
    for vector in vectors:
        pieces.append(small[:, start : start + vector.shape[0]].reshape(-1))
        start += vector.shape[0]
    qv_full, outb_full, upb_full, downb_full, gain_one, shift_one, gain_two, shift_two = pieces
    row_count = seq_count * local_len
    total_len = local_len * lax.axis_size("fsdp")
    offset = lax.axis_index("fsdp") * local_len
    head_count = features // HD
    scale = HD ** (-0.5)
    inputs = tokens.reshape(row_count, features).astype(jnp.float32)
    normal_one, pull_one = jax.vjp(normalize, inputs)
    first = (normal_one * gain_one.astype(jnp.float32) + shift_one.astype(jnp.float32)).astype(
        jnp.bfloat16
    )
    qv_wide = qv_full.astype(jnp.float32)
    zero_keys = jnp.zeros((features,), jnp.float32)
    full_bias = jnp.concatenate([qv_wide[:features], zero_keys, qv_wide[features:]])
    mixed = (jnp.dot(first, qkv_full, preferred_element_type=jnp.float32) + full_bias).astype(
        jnp.bfloat16
    )
    queries = mixed[:, :features].reshape(seq_count, local_len, features)
    keys = mixed[:, features : 2 * features].reshape(seq_count, local_len, features)
    values = mixed[:, 2 * features :].reshape(seq_count, local_len, features)
    keys_all, values_all = (
        lax.all_gather(keys, "fsdp", axis=1, tiled=True),
        lax.all_gather(values, "fsdp", axis=1, tiled=True),
    )
    query_pos = offset + jnp.arange(local_len, dtype=jnp.int32)
    key_pos = jnp.arange(total_len, dtype=jnp.int32)
    allowed = key_pos[None, :] <= query_pos[:, None]

    def head_parts(head_index, source):
        column = head_index * HD
        return lax.dynamic_slice_in_dim(source, column, HD, 2)

    def head_scores(query_part, key_part):
        scores = (
            jnp.einsum("sqd,skd->sqk", query_part, key_part, preferred_element_type=jnp.float32)
            * scale
        )
        return jnp.where(allowed[None], scores, -1e30)

    def head_forward(head_index):
        query_part = head_parts(head_index, queries)
        key_part = head_parts(head_index, keys_all)
        value_part = head_parts(head_index, values_all)
        scores = head_scores(query_part, key_part)
        row_peak = jnp.max(scores, axis=-1, keepdims=True)
        weights = jnp.exp(scores - row_peak)
        row_total = jnp.sum(weights, axis=-1, keepdims=True)
        probabilities = (weights / row_total).astype(jnp.bfloat16)
        head_out = jnp.einsum(
            "sqk,skd->sqd", probabilities, value_part, preferred_element_type=jnp.float32
        )
        return (head_out, (row_peak + jnp.log(row_total))[..., 0])

    head_indices = jnp.arange(head_count, dtype=jnp.int32)
    per_head, logsum = lax.map(head_forward, head_indices)
    attended = per_head.transpose(1, 2, 0, 3).reshape(row_count, features).astype(jnp.bfloat16)
    branch = jnp.dot(attended, out_full, preferred_element_type=jnp.float32) + outb_full.astype(
        jnp.float32
    )
    hidden = inputs + branch
    normal_two, pull_two = jax.vjp(normalize, hidden)
    second = (normal_two * gain_two.astype(jnp.float32) + shift_two.astype(jnp.float32)).astype(
        jnp.bfloat16
    )
    upward = jnp.dot(second, up_full, preferred_element_type=jnp.float32) + upb_full.astype(
        jnp.float32
    )
    activated, pull_gelu = jax.vjp(gelu_exact, upward)
    act_low = activated.astype(jnp.bfloat16)
    result = hidden + (
        jnp.dot(act_low, down_full, preferred_element_type=jnp.float32)
        + downb_full.astype(jnp.float32)
    )
    qkv_back, out_back, up_back, down_back, gain_one_back, gain_two_back = (
        qkv_full,
        out_full,
        up_full,
        down_full,
        gain_one,
        gain_two,
    )
    upstream = cotangent.reshape(row_count, features).astype(jnp.float32)
    down_grad = cotangent.reshape(row_count, features)
    grad_down_w = jnp.einsum("rf,rd->fd", act_low, down_grad, preferred_element_type=jnp.float32)
    grad_down_b = jnp.sum(upstream, axis=0)
    grad_act = jnp.einsum("rd,fd->rf", down_grad, down_back, preferred_element_type=jnp.float32)
    (grad_upward,) = pull_gelu(grad_act)
    up_low = grad_upward.astype(jnp.bfloat16)
    grad_up_w = jnp.einsum("rd,rf->df", second, up_low, preferred_element_type=jnp.float32)
    grad_up_b = jnp.sum(up_low.astype(jnp.float32), axis=0)
    grad_second = jnp.einsum("rf,df->rd", up_low, up_back, preferred_element_type=jnp.float32)
    grad_gain_two = jnp.sum(grad_second * normal_two, axis=0)
    grad_shift_two = jnp.sum(grad_second, axis=0)
    (grad_norm_two,) = pull_two(grad_second * gain_two_back.astype(jnp.float32))
    grad_hidden = upstream + grad_norm_two
    branch_grad = grad_hidden.astype(jnp.bfloat16)
    grad_out_w = jnp.einsum("rc,rd->cd", attended, branch_grad, preferred_element_type=jnp.float32)
    grad_out_b = jnp.sum(branch_grad.astype(jnp.float32), axis=0)
    grad_att = jnp.einsum("rd,cd->rc", branch_grad, out_back, preferred_element_type=jnp.float32)
    grad_att = grad_att.astype(jnp.bfloat16).reshape(seq_count, local_len, features)

    def head_backward(head_pair):
        head_index, head_logsum = head_pair
        query_part = head_parts(head_index, queries)
        key_part = head_parts(head_index, keys_all)
        value_part = head_parts(head_index, values_all)
        grad_part = head_parts(head_index, grad_att)
        scores = head_scores(query_part, key_part)
        probabilities = jnp.exp(scores - head_logsum[..., None])
        grad_probs = jnp.einsum(
            "sqd,skd->sqk", grad_part, value_part, preferred_element_type=jnp.float32
        )
        inner_sum = jnp.sum(probabilities * grad_probs, axis=-1, keepdims=True)
        grad_scores = (probabilities * (grad_probs - inner_sum)).astype(jnp.bfloat16)
        grad_query = (
            jnp.einsum("sqk,skd->sqd", grad_scores, key_part, preferred_element_type=jnp.float32)
            * scale
        )
        grad_key = (
            jnp.einsum("sqk,sqd->skd", grad_scores, query_part, preferred_element_type=jnp.float32)
            * scale
        )
        grad_value = jnp.einsum(
            "sqk,sqd->skd",
            probabilities.astype(jnp.bfloat16),
            grad_part,
            preferred_element_type=jnp.float32,
        )
        return (grad_query, grad_key, grad_value)

    query_grads, key_grads, value_grads = lax.map(head_backward, (head_indices, logsum))
    query_grads = query_grads.transpose(1, 2, 0, 3).reshape(seq_count, local_len, features)
    key_grads = key_grads.transpose(1, 2, 0, 3).reshape(seq_count, total_len, features)
    value_grads = value_grads.transpose(1, 2, 0, 3).reshape(seq_count, total_len, features)
    own_keys, own_values = (
        lax.psum_scatter(key_grads.astype(jnp.bfloat16), "fsdp", scatter_dimension=1, tiled=True),
        lax.psum_scatter(value_grads.astype(jnp.bfloat16), "fsdp", scatter_dimension=1, tiled=True),
    )
    mixed_grad = jnp.concatenate(
        [query_grads.astype(jnp.bfloat16), own_keys, own_values], axis=-1
    )
    mixed_grad = mixed_grad.reshape(row_count, 3 * features)
    grad_qkv_w = jnp.einsum("rd,re->de", first, mixed_grad, preferred_element_type=jnp.float32)
    column_sums = jnp.sum(mixed_grad.astype(jnp.float32), axis=0)
    grad_qv_b = jnp.concatenate([column_sums[:features], column_sums[2 * features :]])
    grad_first = jnp.einsum("re,de->rd", mixed_grad, qkv_back, preferred_element_type=jnp.float32)
    grad_gain_one = jnp.sum(grad_first * normal_one, axis=0)
    grad_shift_one = jnp.sum(grad_first, axis=0)
    (grad_norm_one,) = pull_one(grad_first * gain_one_back.astype(jnp.float32))
    grad_inputs = grad_hidden + grad_norm_one
    fsdp = lax.axis_size("fsdp")

    def grad_units(matrix):
        blocks = matrix.shape[1] // features
        return matrix.astype(jnp.bfloat16).reshape(fsdp, rows, blocks, features).transpose(0, 2, 1, 3)

    def reduce_all(matrix):
        part = lax.psum_scatter(matrix, everyone, scatter_dimension=0, tiled=True)
        return lax.all_gather(part, "rep", axis=0, tiled=True)

    def own_matrix(units):
        blocks = units.shape[0] // rows
        wide = units.reshape(blocks, rows, features).transpose(1, 0, 2)
        return wide.reshape(rows, blocks * features).astype(jnp.float32)

    down_own = reduce_all(grad_down_w.astype(jnp.bfloat16)).astype(jnp.float32)
    up_own = own_matrix(reduce_all(grad_units(grad_up_w).reshape(-1, features)))
    packed = jnp.concatenate([grad_units(grad_qkv_w), grad_units(grad_out_w)], 1)
    one_own = reduce_all(packed.reshape(-1, features))
    qkv_own = own_matrix(one_own[: 3 * rows])
    out_own = own_matrix(one_own[3 * rows :])
    small_grads = (
        grad_qv_b, grad_out_b, grad_up_b, grad_down_b,
        grad_gain_one, grad_shift_one, grad_gain_two, grad_shift_two,
    )
    stacked = jnp.concatenate([g.reshape(fsdp, -1) for g in small_grads], 1)
    stacked = lax.psum(stacked, ("rep", "fsdp"))
    mine = lax.dynamic_index_in_dim(stacked, lax.axis_index("fsdp"), 0, keepdims=False)
    small_own = []
    start = 0
    for g in small_grads:
        width = g.shape[0] // fsdp
        small_own.append(mine[start : start + width])
        start += width
    return (
        result.reshape(seq_count, local_len, features),
        grad_inputs.reshape(seq_count, local_len, features),
        qkv_own,
        small_own[0],
        out_own,
        small_own[1],
        up_own,
        small_own[2],
        down_own,
        small_own[3],
        small_own[4],
        small_own[5],
        small_own[6],
        small_own[7],
    )


def solution(mesh):
    return jax.shard_map(
        local,
        mesh=mesh,
        in_specs=(
            P("rep", "fsdp", None),
            P("fsdp", None),
            P("fsdp"),
            P("fsdp", None),
            P("fsdp"),
            P("fsdp", None),
            P("fsdp"),
            P("fsdp", None),
            P("fsdp"),
            P("fsdp"),
            P("fsdp"),
            P("fsdp"),
            P("fsdp"),
            P("rep", "fsdp", None),
        ),
        out_specs=(
            P("rep", "fsdp", None),
            P("rep", "fsdp", None),
            P("fsdp", None),
            P("fsdp"),
            P("fsdp", None),
            P("fsdp"),
            P("fsdp", None),
            P("fsdp"),
            P("fsdp", None),
            P("fsdp"),
            P("fsdp"),
            P("fsdp"),
            P("fsdp"),
            P("fsdp"),
        ),
        check_vma=False,
    )
```

```python
import numpy as np
import jax
import jax.numpy as jnp
from jax import lax
from jax.experimental import pallas as pl
from jax.experimental.pallas import tpu as pltpu
from jax.sharding import PartitionSpec as P

HD = 64
LANES = 128
EPSILON = 1e-05
F32 = jnp.float32
BF16 = jnp.bfloat16
NT = (((1,), (1,)), ((), ()))
NN = (((1,), (0,)), ((), ()))
TN = (((0,), (0,)), ((), ()))


def dot(left, right, dims):
    return lax.dot_general(left, right, dims, preferred_element_type=F32)


MOVE_A = {
    (0, 0): (0, 0), (0, 1): (0, 1), (0, 3): (1, 0), (0, 2): (1, 1),
    (1, 0): (1, 3), (1, 3): (0, 3), (1, 1): (1, 2), (1, 2): (0, 2),
}
MOVE_B = {
    (0, 0): (1, 0), (0, 1): (1, 1), (0, 3): (0, 0), (0, 2): (0, 1),
    (1, 0): (0, 3), (1, 3): (1, 3), (1, 1): (0, 2), (1, 2): (1, 2),
}


def block_positions():
    spots = {}
    for (_, z), target in MOVE_A.items():
        spots[target] = [2 * z, None]
    for (_, z), target in MOVE_B.items():
        spots[target][1] = 2 * z + 1
    return spots


def task_table():
    spots = block_positions()
    table = np.zeros((2, 4, 18), np.int32)
    for c in range(2):
        for z in range(4):
            members = [(c, z), (1 - c, z), (c, z ^ 1), (1 - c, z ^ 1)]
            slot_of = {}
            for j, member in enumerate(members):
                for half in range(2):
                    slot_of[spots[member][half]] = 2 * j + half
            mine = spots[(c, z)]
            low, high = (0, 1) if mine[0] < mine[1] else (1, 0)
            tasks = [(low, slot_of[mine[low]]), (high, slot_of[mine[high]])]
            tasks += [(high, slot_of[k]) for k in range(4)]
            tasks += [(low, slot_of[k]) for k in range(mine[low])]
            tasks += [(high, slot_of[k]) for k in range(4, mine[high])]
            table[c, z] = [v for pair in tasks for v in pair]
    return table


TASKS = 9


def both_heads(block):
    lane = lax.broadcasted_iota(jnp.int32, block.shape, 1)
    zero = jnp.zeros_like(block)
    return jnp.concatenate(
        [jnp.where(lane < HD, block, zero), jnp.where(lane < HD, zero, block)], 0
    )


def pick_heads(wide, half):
    row = lax.broadcasted_iota(jnp.int32, (LANES, half), 0)
    return jnp.where(row < HD, wide[:, :half], wide[:, half:])


def spread_keys(parts, scratch, half):
    for j, part in enumerate(parts):
        scratch[2 * j] = part[0, :half, :]
        scratch[2 * j + 1] = part[0, half:, :]


def attend_forward(tab, q, k0, k1, k2, k3, v0, v1, v2, v3, out, lse, keys, values_t, queries, scores):
    half = q.shape[1] // 2
    wide = 2 * half
    spread_keys((k0, k1, k2, k3), keys, half)
    for j, part in enumerate((v0, v1, v2, v3)):
        values_t[2 * j] = part[0, :half, :].T
        values_t[2 * j + 1] = part[0, half:, :].T
    scale = jnp.asarray(HD ** (-0.5), BF16)
    for h in range(2):
        queries[h] = both_heads(q[0, h * half : (h + 1) * half, :] * scale)
    key_at = lax.broadcasted_iota(jnp.int32, (half, wide), 0)
    query_at = lax.broadcasted_iota(jnp.int32, (half, wide), 1)
    query_at = jnp.where(query_at < half, query_at, query_at - half)
    low = tab[0]
    high = tab[2]
    peaks = []
    for t in range(TASKS):
        part = dot(keys[tab[2 * t + 1]], queries[tab[2 * t]], NT)
        if t < 2:
            part = jnp.where(key_at <= query_at, part, -1e30)
        scores[t] = part
        peaks.append(jnp.max(part, 0, keepdims=True))
    peak_low = peaks[0]
    peak_high = peaks[1]
    for t in range(2, 6):
        peak_high = jnp.maximum(peak_high, peaks[t])
    is_low = [None] * TASKS
    for t in range(6, TASKS):
        is_low[t] = tab[2 * t] == low
        peak_low = jnp.where(is_low[t], jnp.maximum(peak_low, peaks[t]), peak_low)
        peak_high = jnp.where(is_low[t], peak_high, jnp.maximum(peak_high, peaks[t]))
    total = {0: 0.0, 1: 0.0}
    accum = {0: 0.0, 1: 0.0}
    for t in range(TASKS):
        if t == 0:
            peak = peak_low
        elif t < 6:
            peak = peak_high
        else:
            peak = jnp.where(is_low[t], peak_low, peak_high)
        weights = jnp.exp(scores[t] - peak)
        part_sum = jnp.sum(weights, 0, keepdims=True)
        part_out = dot(values_t[tab[2 * t + 1]], weights.astype(BF16), NN)
        if t == 0:
            total[0] += part_sum
            accum[0] += part_out
        elif t < 6:
            total[1] += part_sum
            accum[1] += part_out
        else:
            total[0] += jnp.where(is_low[t], part_sum, 0.0)
            total[1] += jnp.where(is_low[t], 0.0, part_sum)
            accum[0] += jnp.where(is_low[t], part_out, 0.0)
            accum[1] += jnp.where(is_low[t], 0.0, part_out)
    for which, (spot, peak) in enumerate(((low, peak_low), (high, peak_high))):
        picked = pick_heads(accum[which] / total[which], half)
        out[pl.ds(pl.multiple_of(spot * half, half), half), :] = picked.T.astype(BF16)
        lse[0, spot] = peak + jnp.log(total[which])


def attend_backward(
    tab, q, k0, k1, k2, k3, v0, v1, v2, v3, att, grad, lse,
    dq, dk0, dk1, dk2, dk3, dv0, dv1, dv2, dv3,
    keys, keys_t, values, queries, grads, deltas, key_sums, value_sums, query_sums,
):
    half = q.shape[1] // 2
    wide = 2 * half
    spread_keys((k0, k1, k2, k3), keys, half)
    spread_keys((v0, v1, v2, v3), values, half)
    for slot in range(8):
        keys_t[slot] = keys[slot].T
    scale = jnp.asarray(HD ** (-0.5), BF16)
    for h in range(2):
        rows = slice(h * half, (h + 1) * half)
        queries[h] = both_heads(q[0, rows, :] * scale)
        grads[h] = both_heads(grad[rows, :])
        product = (att[rows, :].astype(F32) * grad[rows, :].astype(F32)).T
        deltas[h] = jnp.concatenate(
            [jnp.sum(product[:HD], 0, keepdims=True), jnp.sum(product[HD:], 0, keepdims=True)], 1
        )
    key_sums[...] = jnp.zeros_like(key_sums)
    value_sums[...] = jnp.zeros_like(value_sums)
    query_sums[...] = jnp.zeros_like(query_sums)
    key_at = lax.broadcasted_iota(jnp.int32, (half, wide), 0)
    query_at = lax.broadcasted_iota(jnp.int32, (half, wide), 1)
    query_at = jnp.where(query_at < half, query_at, query_at - half)
    for t in range(TASKS):
        at = tab[2 * t]
        slot = tab[2 * t + 1]
        query = queries[at]
        upstream = grads[at]
        part = dot(keys[slot], query, NT)
        if t < 2:
            part = jnp.where(key_at <= query_at, part, -1e30)
        probs = jnp.exp(part - lse[0, at])
        grad_probs = dot(values[slot], upstream, NT)
        grad_scores = (probs * (grad_probs - deltas[at])).astype(BF16)
        value_sums[slot] += dot(probs.astype(BF16), upstream, NN)
        key_sums[slot] += dot(grad_scores, query, NN)
        query_sums[at] += dot(keys_t[slot], grad_scores, NN)
    for h in range(2):
        picked = pick_heads(query_sums[h], half) * (HD ** (-0.5))
        dq[h * half : (h + 1) * half, :] = picked.T.astype(BF16)
    for j, (dk, dv) in enumerate(((dk0, dv0), (dk1, dv1), (dk2, dv2), (dk3, dv3))):
        for h in range(2):
            rows = slice(h * half, (h + 1) * half)
            dk[rows, :] = key_sums[2 * j + h].astype(dk.dtype)
            dv[rows, :] = value_sums[2 * j + h].astype(dv.dtype)


def call(kernel, name, grid, in_specs, out_specs, out_shape, scratch=(), prefetch=0):
    return pl.pallas_call(
        kernel,
        name=name,
        grid_spec=pltpu.PrefetchScalarGridSpec(
            num_scalar_prefetch=prefetch,
            grid=grid,
            in_specs=in_specs,
            out_specs=out_specs,
            scratch_shapes=list(scratch),
        ),
        out_shape=out_shape,
        compiler_params=pltpu.CompilerParams(
            dimension_semantics=("arbitrary",) * len(grid), vmem_limit_bytes=60 * 1024 * 1024
        ),
    )


def whole(shape):
    return pl.BlockSpec(shape, lambda *_: (0,) * len(shape))


def sds(shape, dtype):
    return jax.ShapeDtypeStruct(shape, dtype)


def attention_forward(table, mixed, others):
    _, length, width = mixed.shape
    pairs = width // LANES
    half = length // 2

    def column(which):
        return pl.BlockSpec((1, length, LANES), lambda p, tab: (which, 0, p))

    return call(
        attend_forward,
        "attend_forward",
        (pairs,),
        [column(0), column(1)] + [column(0)] * 3 + [column(2)] + [column(1)] * 3,
        [
            pl.BlockSpec((length, LANES), lambda p, tab: (0, p)),
            pl.BlockSpec((1, 2, 1, length), lambda p, tab: (p, 0, 0, 0)),
        ],
        [sds((length, width), BF16), sds((pairs, 2, 1, length), F32)],
        [
            pltpu.VMEM((8, half, LANES), BF16),
            pltpu.VMEM((8, LANES, half), BF16),
            pltpu.VMEM((2, length, LANES), BF16),
            pltpu.VMEM((TASKS, half, length), F32),
        ],
        prefetch=1,
    )(table, mixed, mixed, *others, mixed, *others)


def attention_backward(table, mixed, others, attended, grad_att, lse):
    _, length, width = mixed.shape
    pairs = width // LANES
    half = length // 2

    def column(which):
        return pl.BlockSpec((1, length, LANES), lambda p, tab: (which, 0, p))

    flat = pl.BlockSpec((length, LANES), lambda p, tab: (0, p))
    own = [sds((length, width), F32)]
    sent = [sds((length, width), BF16)] * 3
    return call(
        attend_backward,
        "attend_backward",
        (pairs,),
        [column(0), column(1)]
        + [column(0)] * 3
        + [column(2)]
        + [column(1)] * 3
        + [flat, flat, pl.BlockSpec((1, 2, 1, length), lambda p, tab: (p, 0, 0, 0))],
        [flat] * 9,
        [sds((length, width), BF16)] + own + sent + own + sent,
        [
            pltpu.VMEM((8, half, LANES), BF16),
            pltpu.VMEM((8, LANES, half), BF16),
            pltpu.VMEM((8, half, LANES), BF16),
            pltpu.VMEM((2, length, LANES), BF16),
            pltpu.VMEM((2, length, LANES), BF16),
            pltpu.VMEM((2, 1, length), F32),
            pltpu.VMEM((8, half, LANES), F32),
            pltpu.VMEM((8, half, LANES), F32),
            pltpu.VMEM((2, LANES, length), F32),
        ],
        prefetch=1,
    )(table, mixed, mixed, *others, mixed, *others, attended, grad_att, lse)


def normal_parts(rows):
    centre = rows - jnp.mean(rows, -1, keepdims=True)
    inverse = lax.rsqrt(jnp.mean(centre * centre, -1, keepdims=True) + EPSILON)
    return centre * inverse, inverse


def normal_pull(normal, inverse, grad):
    mean_grad = jnp.mean(grad, -1, keepdims=True)
    mean_both = jnp.mean(grad * normal, -1, keepdims=True)
    return inverse * (grad - mean_grad - normal * mean_both)


def square(block):
    return block[...].reshape(-1, block.shape[-1])


def enter_kernel(x, gain, shift, weight, bias, first, mixed):
    width = mixed.shape[-1]
    features = x.shape[-1]

    @pl.when(pl.program_id(0) == 0)
    def _():
        normal, _ = normal_parts(x[...].astype(F32))
        first[...] = (normal * gain[...] + shift[...]).astype(BF16)

    made = dot(first[...], square(weight), NN) + bias[0]
    mixed[0, :, :features] = made.astype(BF16)
    mixed[0, :, features:] = jnp.zeros((x.shape[0], width - features), BF16)


def enter(x, gain, shift, units, bias):
    length, features = x.shape
    width = -(-features // LANES) * LANES
    unit = (units.shape[0], 1) + units.shape[2:]
    return call(
        enter_kernel,
        "enter",
        (3,),
        [
            whole(x.shape),
            whole((1, features)),
            whole((1, features)),
            pl.BlockSpec(unit, lambda u: (0, u, 0, 0)),
            pl.BlockSpec((1, 1, features), lambda u: (u, 0, 0)),
        ],
        [whole(x.shape), pl.BlockSpec((1, length, width), lambda u: (u, 0, 0))],
        [sds(x.shape, BF16), sds((3, length, width), BF16)],
    )(x, gain, shift, units, bias)


def project_kernel(x, attended, weight, bias, gain, shift, hidden, second):
    features = x.shape[-1]
    branch = dot(attended[:, :features], square(weight), NN) + bias[...]
    stream = x[...].astype(F32) + branch
    hidden[...] = stream
    normal, _ = normal_parts(stream)
    second[...] = (normal * gain[...] + shift[...]).astype(BF16)


def project(x, attended, units, bias, gain, shift):
    length, features = x.shape
    unit = (units.shape[0], 1) + units.shape[2:]
    row = whole((1, features))
    return call(
        project_kernel,
        "project",
        (1,),
        [whole(x.shape), whole(attended.shape), pl.BlockSpec(unit, lambda u: (0, 3, 0, 0)), row, row, row],
        [whole(x.shape), whole(x.shape)],
        [sds(x.shape, F32), sds(x.shape, BF16)],
    )(x, attended, units, bias, gain, shift)


def feed_kernel(
    hidden, second, cot, up, down, up_bias, down_bias,
    result, up_grad, down_grad, up_bias_grad, second_grad, total,
):
    step = pl.program_id(0)
    wide_up = square(up)
    upward = dot(second[...], wide_up, NN) + up_bias[0]
    bell = 0.5 * (1.0 + lax.erf(upward * (0.5**0.5)))
    active = (upward * bell).astype(BF16)
    slope = bell + upward * jnp.exp(-0.5 * upward * upward) * ((0.5 / np.pi) ** 0.5)
    grad_up = (slope * dot(cot[...], down[...], NT)).astype(BF16)
    out_part = dot(active, down[...], NN)
    back_part = dot(grad_up, wide_up, NT)
    down_grad[...] = dot(active, cot[...], TN).astype(BF16)
    up_grad[...] = dot(second[...], grad_up, TN).astype(BF16).reshape(up_grad.shape)
    up_bias_grad[0] = jnp.sum(grad_up.astype(F32), 0, keepdims=True)

    @pl.when(step == 0)
    def _():
        total[...] = hidden[...] + down_bias[...] + out_part
        second_grad[...] = back_part

    @pl.when(step > 0)
    def _():
        total[...] += out_part
        second_grad[...] += back_part

    @pl.when(step == pl.num_programs(0) - 1)
    def _():
        result[...] = total[...].astype(result.dtype)


def feed(hidden, second, cot, up_units, down_full, up_bias, down_bias):
    length, features = hidden.shape
    blocks = up_units.shape[1]
    unit = (up_units.shape[0], 1) + up_units.shape[2:]
    up_spec = pl.BlockSpec(unit, lambda b: (0, b, 0, 0))
    down_spec = pl.BlockSpec((features, features), lambda b: (b, 0))
    row_spec = pl.BlockSpec((1, 1, features), lambda b: (b, 0, 0))
    flat = whole(hidden.shape)
    return call(
        feed_kernel,
        "feed",
        (blocks,),
        [flat, flat, flat, up_spec, down_spec, row_spec, whole((1, features))],
        [flat, up_spec, down_spec, row_spec, flat],
        [
            sds(hidden.shape, BF16),
            sds(up_units.shape, BF16),
            sds(down_full.shape, BF16),
            sds((blocks, 1, features), F32),
            sds(hidden.shape, F32),
        ],
        [pltpu.VMEM(hidden.shape, F32)],
    )(hidden, second, cot, up_units, down_full, up_bias, down_bias)


def turn_kernel(second_grad, hidden, cot, attended, weight, gain, stream_grad, att_grad, out_grad, sums):
    features = hidden.shape[-1]
    width = attended.shape[-1]
    normal, inverse = normal_parts(hidden[...])
    upstream = cot[...].astype(F32)
    grad = second_grad[...]
    stream = upstream + normal_pull(normal, inverse, grad * gain[...])
    stream_grad[...] = stream
    low = stream.astype(BF16)
    made = dot(low, square(weight), NT)
    att_grad[:, :features] = made.astype(BF16)
    att_grad[:, features:] = jnp.zeros((hidden.shape[0], width - features), BF16)
    out_grad[...] = dot(attended[:, :features], low, TN).astype(BF16).reshape(out_grad.shape)
    sums[...] = jnp.concatenate(
        [
            jnp.sum(grad * normal, 0, keepdims=True),
            jnp.sum(grad, 0, keepdims=True),
            jnp.sum(low.astype(F32), 0, keepdims=True),
            jnp.sum(upstream, 0, keepdims=True),
            jnp.zeros((4, features), F32),
        ],
        0,
    )


def turn(second_grad, hidden, cot, attended, units, gain):
    length, features = hidden.shape
    unit = (units.shape[0], 1) + units.shape[2:]
    flat = whole(hidden.shape)
    return call(
        turn_kernel,
        "turn",
        (1,),
        [flat, flat, flat, whole(attended.shape), pl.BlockSpec(unit, lambda u: (0, 3, 0, 0)), whole((1, features))],
        [flat, whole(attended.shape), whole(unit), whole((8, features))],
        [sds(hidden.shape, F32), sds(attended.shape, BF16), sds(unit, BF16), sds((8, features), F32)],
    )(second_grad, hidden, cot, attended, units, gain)


def leave_kernel(mixed_grad, first, x, stream_grad, weight, gain, out_grad, token_grad, unit_grad, column_sums, sums, total):
    step = pl.program_id(0)
    features = x.shape[-1]

    @pl.when(step == 3)
    def _():
        unit_grad[...] = out_grad[...]
        normal, inverse = normal_parts(x[...].astype(F32))
        grad = total[...]
        token_grad[...] = (stream_grad[...] + normal_pull(normal, inverse, grad * gain[...])).astype(BF16)
        sums[...] = jnp.concatenate(
            [jnp.sum(grad * normal, 0, keepdims=True), jnp.sum(grad, 0, keepdims=True), jnp.zeros((6, features), F32)], 0
        )
        column_sums[...] = jnp.zeros_like(column_sums)

    @pl.when(step < 3)
    def _():
        grad = mixed_grad[0, :, :features]
        part = dot(grad, square(weight), NT)
        unit_grad[...] = dot(first[...], grad, TN).astype(BF16).reshape(unit_grad.shape)
        column_sums[0] = jnp.sum(grad.astype(F32), 0, keepdims=True)

        @pl.when(step == 0)
        def _():
            total[...] = part

        @pl.when(step > 0)
        def _():
            total[...] += part


def leave(mixed_grad, first, x, stream_grad, units, gain, out_grad):
    length, features = x.shape
    unit = (units.shape[0], 1) + units.shape[2:]
    flat = whole(x.shape)
    return call(
        leave_kernel,
        "leave",
        (4,),
        [
            pl.BlockSpec((1,) + mixed_grad.shape[1:], lambda u: (jnp.minimum(u, 2), 0, 0)),
            flat,
            flat,
            flat,
            pl.BlockSpec(unit, lambda u: (0, jnp.minimum(u, 2), 0, 0)),
            whole((1, features)),
            whole(unit),
        ],
        [
            flat,
            pl.BlockSpec(unit, lambda u: (0, u, 0, 0)),
            pl.BlockSpec((1, 1, features), lambda u: (u, 0, 0)),
            whole((8, features)),
        ],
        [
            sds(x.shape, BF16),
            sds(units.shape, BF16),
            sds((4, 1, features), F32),
            sds((8, features), F32),
        ],
        [pltpu.VMEM(x.shape, F32)],
    )(mixed_grad, first, x, stream_grad, units, gain, out_grad)


def local(
    tokens, w_qkv, qv_bias, w_out, out_bias, w_up, up_bias, w_down, down_bias,
    ln1_gain, ln1_bias, ln2_gain, ln2_bias, cotangent,
):
    _, length, features = tokens.shape
    rows = w_qkv.shape[0]
    half = length // 2
    reps = lax.axis_size("rep")
    fsdp = lax.axis_size("fsdp")
    rep_at = lax.axis_index("rep")
    z_at = lax.axis_index("fsdp")
    everyone = ("fsdp", "rep")
    grid = ("rep", "fsdp")

    def links(move):
        out = []
        for rep in range(reps):
            for z in range(fsdp):
                parity, target = move(rep % 2, z)
                out.append((rep * fsdp + z, (rep - rep % 2 + parity) * fsdp + target))
        return out

    def turned(perm):
        return [(b, a) for a, b in perm]

    move_a = links(lambda c, z: MOVE_A[(c, z)])
    move_b = links(lambda c, z: MOVE_B[(c, z)])
    to_core = links(lambda c, z: (1 - c, z))
    to_z = links(lambda c, z: (c, z ^ 1))

    def send(value, perm):
        return lax.ppermute(value, grid, perm)

    def swap(value):
        return jnp.concatenate([send(value[:half], move_a), send(value[half:], move_b)], 0)

    def swap_back(value):
        return jnp.concatenate(
            [send(value[:half], turned(move_a)), send(value[half:], turned(move_b))], 0
        )

    table = lax.dynamic_slice(
        jnp.asarray(task_table().reshape(8, -1)), (rep_at % 2 * 4 + z_at, 0), (1, 18)
    ).reshape(-1)

    def own_piece(matrix):
        part = matrix.shape[0] // reps
        return lax.dynamic_slice_in_dim(matrix, rep_at * part, part, 0)

    def to_units(matrix):
        blocks = matrix.shape[1] // features
        return [matrix[:, b * features : (b + 1) * features] for b in range(blocks)]

    def gather_all(matrix):
        return lax.all_gather(own_piece(matrix), everyone, axis=0, tiled=True)

    x = swap(tokens[0])
    cot = swap(cotangent[0])
    units_one = gather_all(jnp.concatenate(to_units(w_qkv) + [w_out], 0)).reshape(fsdp, 4, rows, features)
    units_up = gather_all(jnp.concatenate(to_units(w_up), 0)).reshape(fsdp, -1, rows, features)
    down_full = gather_all(w_down)
    vectors = (qv_bias, out_bias, up_bias, down_bias, ln1_gain, ln1_bias, ln2_gain, ln2_bias)
    small = lax.all_gather(jnp.concatenate(vectors), "fsdp", axis=0).astype(F32)
    pieces = []
    start = 0
    for vector in vectors:
        pieces.append(small[:, start : start + vector.shape[0]].reshape(1, -1))
        start += vector.shape[0]
    qv_full, outb_full, upb_full, downb_full, gain_one, shift_one, gain_two, shift_two = pieces
    bias = jnp.stack([qv_full[:, :features], jnp.zeros((1, features), F32), qv_full[:, features:]])

    first, mixed = enter(x, gain_one, shift_one, units_one, bias)
    pair = mixed[1:]
    from_core = send(pair, to_core)
    from_z = send(pair, to_z)
    others = (from_core, from_z, send(from_z, to_core))
    attended, lse = attention_forward(table, mixed, others)
    hidden, second = project(x, attended, units_one, outb_full, gain_two, shift_two)
    result, up_grad, down_grad, up_bias_grad, second_grad = feed(
        hidden, second, cot, units_up, down_full, upb_full.reshape(-1, 1, features), downb_full
    )
    layer_out = swap_back(result).astype(F32)
    stream_grad, att_grad, out_grad, sums_two = turn(second_grad, hidden, cot, attended, units_one, gain_two)
    att_grad, up_grad, down_grad = lax.optimization_barrier((att_grad, up_grad, down_grad))

    def reduce_part(matrix):
        return lax.psum_scatter(matrix.reshape(-1, features), everyone, scatter_dimension=0, tiled=True)

    def spread_part(part):
        return lax.all_gather(part, "rep", axis=0, tiled=True)

    down_own = spread_part(reduce_part(down_grad)).astype(F32)
    up_own = spread_part(reduce_part(up_grad))

    dq, *rest = attention_backward(table, mixed, others, attended, att_grad, lse)
    dk, dv = rest[:4], rest[4:]
    core_got = [send(jnp.stack([dk[1], dv[1]]), to_core), send(jnp.stack([dk[3], dv[3]]), to_core)]
    z_sum = (jnp.stack([dk[2], dv[2]]).astype(F32) + core_got[1].astype(F32)).astype(BF16)
    z_got = send(z_sum, to_z)
    own = jnp.stack([dk[0], dv[0]]) + core_got[0].astype(F32) + z_got.astype(F32)
    mixed_grad = jnp.concatenate([dq[None], own.astype(BF16)], 0)
    token_low, one_grad, column_sums, sums_one = leave(
        mixed_grad, first, x, stream_grad, units_one, gain_one, out_grad
    )
    grad_tokens = swap_back(token_low).astype(F32)
    one_own = spread_part(reduce_part(one_grad))

    def side_by_side(stack):
        return jnp.concatenate(list(stack), 1).astype(F32)

    up_own = side_by_side(up_own.reshape(-1, rows, features))
    one_own = one_own.reshape(4, rows, features)
    qkv_own = side_by_side(one_own[:3])
    out_own = one_own[3].astype(F32)
    small_grads = (
        jnp.concatenate([column_sums[0], column_sums[2]], 1),
        sums_two[2], up_bias_grad, sums_two[3],
        sums_one[0], sums_one[1], sums_two[0], sums_two[1],
    )
    stacked = jnp.concatenate([g.reshape(fsdp, -1) for g in small_grads], 1)
    stacked = lax.psum(stacked, grid)
    mine = lax.dynamic_index_in_dim(stacked, z_at, 0, keepdims=False)
    small_own = []
    start = 0
    for g in small_grads:
        width = g.size // fsdp
        small_own.append(mine[start : start + width])
        start += width
    return (
        layer_out[None], grad_tokens[None],
        qkv_own, small_own[0], out_own, small_own[1],
        up_own, small_own[2], down_own, small_own[3],
        small_own[4], small_own[5], small_own[6], small_own[7],
    )


def solution(mesh):
    data = P("rep", "fsdp", None)
    matrix = P("fsdp", None)
    vector = P("fsdp")
    return jax.shard_map(
        local,
        mesh=mesh,
        in_specs=(
            data, matrix, vector, matrix, vector, matrix, vector, matrix, vector,
            vector, vector, vector, vector, data,
        ),
        out_specs=(
            data, data, matrix, vector, matrix, vector, matrix, vector, matrix, vector,
            vector, vector, vector, vector,
        ),
        check_vma=False,
    )
```

```python
import functools

import numpy as np
import jax
import jax.numpy as jnp
from jax import lax
from jax.experimental import pallas as pl
from jax.experimental.pallas import tpu as pltpu
from jax.sharding import PartitionSpec as P


HD = 64
LANES = 128
EPSILON = 1e-05
F32 = jnp.float32
BF16 = jnp.bfloat16
NT = (((1,), (1,)), ((), ()))
NN = (((1,), (0,)), ((), ()))
TN = (((0,), (0,)), ((), ()))


def dot(left, right, dims):
    return lax.dot_general(left, right, dims, preferred_element_type=F32)


def owner(block):
    return min(block, 7 - block)


def destination(pick, z, half):
    index = owner(2 * z + half)
    return index % 2, index // 2 if pick == 0 else 3 - index // 2


def task_table():
    def held(index):
        return [b for h in range(2) for b in range(h, 8, 2) if owner(b) == index]

    table = np.zeros((4, 18), np.int32)
    for me in range(4):
        slot_of = {}
        for j, member in enumerate((me, me ^ 1, me ^ 2, me ^ 3)):
            for half in range(2):
                slot_of[held(member)[half]] = 2 * j + half
        mine = held(me)
        low, high = (0, 1) if mine[0] < mine[1] else (1, 0)
        tasks = [(low, slot_of[mine[low]]), (high, slot_of[mine[high]])]
        tasks += [(high, slot_of[k]) for k in range(4)]
        tasks += [(low, slot_of[k]) for k in range(mine[low])]
        tasks += [(high, slot_of[k]) for k in range(4, mine[high])]
        table[me] = [v for pair in tasks for v in pair]
    return table


TASKS = 9


def both_heads(block):
    lane = lax.broadcasted_iota(jnp.int32, block.shape, 1)
    zero = jnp.zeros_like(block)
    return jnp.concatenate(
        [jnp.where(lane < HD, block, zero), jnp.where(lane < HD, zero, block)], 0
    )


def pick_heads(wide, half):
    row = lax.broadcasted_iota(jnp.int32, (LANES, half), 0)
    return jnp.where(row < HD, wide[:, :half], wide[:, half:])


def spread_keys(parts, scratch, half):
    for j, part in enumerate(parts):
        scratch[2 * j] = part[0, :half, :]
        scratch[2 * j + 1] = part[0, half:, :]


def attend_forward(tab, q, k0, k1, k2, k3, v0, v1, v2, v3, out, lse, keys, values_t, queries, scores):
    half = q.shape[0] // 2
    wide = 2 * half
    spread_keys((k0, k1, k2, k3), keys, half)
    for j, part in enumerate((v0, v1, v2, v3)):
        values_t[2 * j] = part[0, :half, :].T
        values_t[2 * j + 1] = part[0, half:, :].T
    scale = jnp.asarray(HD ** (-0.5), BF16)
    for h in range(2):
        queries[h] = both_heads(q[h * half : (h + 1) * half, :] * scale)
    key_at = lax.broadcasted_iota(jnp.int32, (half, wide), 0)
    query_at = lax.broadcasted_iota(jnp.int32, (half, wide), 1)
    query_at = jnp.where(query_at < half, query_at, query_at - half)
    low = tab[0]
    high = tab[2]
    peaks = []
    for t in range(TASKS):
        part = dot(keys[tab[2 * t + 1]], queries[tab[2 * t]], NT)
        if t < 2:
            part = jnp.where(key_at <= query_at, part, -1e30)
        scores[t] = part
        peaks.append(jnp.max(part, 0, keepdims=True))
    peak_low = peaks[0]
    peak_high = peaks[1]
    for t in range(2, 6):
        peak_high = jnp.maximum(peak_high, peaks[t])
    is_low = [None] * TASKS
    for t in range(6, TASKS):
        is_low[t] = tab[2 * t] == low
        peak_low = jnp.where(is_low[t], jnp.maximum(peak_low, peaks[t]), peak_low)
        peak_high = jnp.where(is_low[t], peak_high, jnp.maximum(peak_high, peaks[t]))
    total = {0: 0.0, 1: 0.0}
    accum = {0: 0.0, 1: 0.0}
    for t in range(TASKS):
        if t == 0:
            peak = peak_low
        elif t < 6:
            peak = peak_high
        else:
            peak = jnp.where(is_low[t], peak_low, peak_high)
        weights = jnp.exp(scores[t] - peak)
        part_sum = jnp.sum(weights, 0, keepdims=True)
        part_out = dot(values_t[tab[2 * t + 1]], weights.astype(BF16), NN)
        if t == 0:
            total[0] += part_sum
            accum[0] += part_out
        elif t < 6:
            total[1] += part_sum
            accum[1] += part_out
        else:
            total[0] += jnp.where(is_low[t], part_sum, 0.0)
            total[1] += jnp.where(is_low[t], 0.0, part_sum)
            accum[0] += jnp.where(is_low[t], part_out, 0.0)
            accum[1] += jnp.where(is_low[t], 0.0, part_out)
    for which, (spot, peak) in enumerate(((low, peak_low), (high, peak_high))):
        picked = pick_heads(accum[which] / total[which], half)
        out[pl.ds(pl.multiple_of(spot * half, half), half), :] = picked.T.astype(BF16)
        lse[0, spot] = peak + jnp.log(total[which])


def attend_backward(
    tab, q, k0, k1, k2, k3, v0, v1, v2, v3, att, grad, lse,
    dq, pair0, pair1, pair2, pair3,
    keys, keys_t, values, queries, grads, deltas, key_sums, value_sums, query_sums,
):
    half = q.shape[0] // 2
    wide = 2 * half
    spread_keys((k0, k1, k2, k3), keys, half)
    spread_keys((v0, v1, v2, v3), values, half)
    for slot in range(8):
        keys_t[slot] = keys[slot].T
    scale = jnp.asarray(HD ** (-0.5), BF16)
    for h in range(2):
        rows = slice(h * half, (h + 1) * half)
        queries[h] = both_heads(q[rows, :] * scale)
        grads[h] = both_heads(grad[rows, :])
        product = (att[rows, :].astype(F32) * grad[rows, :].astype(F32)).T
        deltas[h] = jnp.concatenate(
            [jnp.sum(product[:HD], 0, keepdims=True), jnp.sum(product[HD:], 0, keepdims=True)], 1
        )
    key_sums[...] = jnp.zeros_like(key_sums)
    value_sums[...] = jnp.zeros_like(value_sums)
    query_sums[...] = jnp.zeros_like(query_sums)
    key_at = lax.broadcasted_iota(jnp.int32, (half, wide), 0)
    query_at = lax.broadcasted_iota(jnp.int32, (half, wide), 1)
    query_at = jnp.where(query_at < half, query_at, query_at - half)
    for t in range(TASKS):
        at = tab[2 * t]
        slot = tab[2 * t + 1]
        query = queries[at]
        upstream = grads[at]
        part = dot(keys[slot], query, NT)
        if t < 2:
            part = jnp.where(key_at <= query_at, part, -1e30)
        probs = jnp.exp(part - lse[0, at])
        grad_probs = dot(values[slot], upstream, NT)
        grad_scores = (probs * (grad_probs - deltas[at])).astype(BF16)
        value_sums[slot] += dot(probs.astype(BF16), upstream, NN)
        key_sums[slot] += dot(grad_scores, query, NN)
        query_sums[at] += dot(keys_t[slot], grad_scores, NN)
    for h in range(2):
        picked = pick_heads(query_sums[h], half) * (HD ** (-0.5))
        dq[h * half : (h + 1) * half, :] = picked.T.astype(BF16)
    for j, pair in enumerate((pair0, pair1, pair2, pair3)):
        for h in range(2):
            rows = slice(h * half, (h + 1) * half)
            pair[0, rows, :] = key_sums[2 * j + h].astype(pair.dtype)
            pair[1, rows, :] = value_sums[2 * j + h].astype(pair.dtype)


def call(kernel, grid, in_specs, out_specs, out_shape, scratch=(), prefetch=0):
    return pl.pallas_call(
        kernel,
        grid_spec=pltpu.PrefetchScalarGridSpec(
            num_scalar_prefetch=prefetch,
            grid=grid,
            in_specs=in_specs,
            out_specs=out_specs,
            scratch_shapes=list(scratch),
        ),
        out_shape=out_shape,
        compiler_params=pltpu.CompilerParams(
            dimension_semantics=("arbitrary",) * len(grid), vmem_limit_bytes=60 * 1024 * 1024
        ),
    )


def whole(shape):
    return pl.BlockSpec(shape, lambda *_: (0,) * len(shape))


def sds(shape, dtype):
    return jax.ShapeDtypeStruct(shape, dtype)


def attention_inputs(queries, pair, others):
    length, _ = queries.shape

    def column(which):
        return pl.BlockSpec((1, length, LANES), lambda p, tab: (which, 0, p))

    flat = pl.BlockSpec((length, LANES), lambda p, tab: (0, p))
    return [flat] + [column(0)] * 4 + [column(1)] * 4, (queries, pair, *others, pair, *others)


def attention_forward(table, queries, pair, others):
    length, width = queries.shape
    pairs = width // LANES
    half = length // 2
    specs, operands = attention_inputs(queries, pair, others)
    return call(
        attend_forward,
        (pairs,),
        specs,
        [
            pl.BlockSpec((length, LANES), lambda p, tab: (0, p)),
            pl.BlockSpec((1, 2, 1, length), lambda p, tab: (p, 0, 0, 0)),
        ],
        [sds((length, width), BF16), sds((pairs, 2, 1, length), F32)],
        [
            pltpu.VMEM((8, half, LANES), BF16),
            pltpu.VMEM((8, LANES, half), BF16),
            pltpu.VMEM((2, length, LANES), BF16),
            pltpu.VMEM((TASKS, half, length), F32),
        ],
        prefetch=1,
    )(table, *operands)


def attention_backward(table, queries, pair, others, attended, grad_att, lse):
    length, width = queries.shape
    pairs = width // LANES
    half = length // 2
    specs, operands = attention_inputs(queries, pair, others)
    flat = pl.BlockSpec((length, LANES), lambda p, tab: (0, p))
    both = pl.BlockSpec((2, length, LANES), lambda p, tab: (0, 0, p))
    return call(
        attend_backward,
        (pairs,),
        specs + [flat, flat, pl.BlockSpec((1, 2, 1, length), lambda p, tab: (p, 0, 0, 0))],
        [flat] + [both] * 4,
        [sds((length, width), BF16), sds((2, length, width), F32)] + [sds((2, length, width), BF16)] * 3,
        [
            pltpu.VMEM((8, half, LANES), BF16),
            pltpu.VMEM((8, LANES, half), BF16),
            pltpu.VMEM((8, half, LANES), BF16),
            pltpu.VMEM((2, length, LANES), BF16),
            pltpu.VMEM((2, length, LANES), BF16),
            pltpu.VMEM((2, 1, length), F32),
            pltpu.VMEM((8, half, LANES), F32),
            pltpu.VMEM((8, half, LANES), F32),
            pltpu.VMEM((2, LANES, length), F32),
        ],
        prefetch=1,
    )(table, *operands, attended, grad_att, lse)


def normal_parts(rows):
    centre = rows - jnp.mean(rows, -1, keepdims=True)
    inverse = lax.rsqrt(jnp.mean(centre * centre, -1, keepdims=True) + EPSILON)
    return centre * inverse, inverse


def normal_pull(normal, inverse, grad):
    mean_grad = jnp.mean(grad, -1, keepdims=True)
    mean_both = jnp.mean(grad * normal, -1, keepdims=True)
    return inverse * (grad - mean_grad - normal * mean_both)


def square(block):
    return block[...].reshape(-1, block.shape[-1])


CHUNK_STARTS = (0, 72, 136, 200)
CHUNK = 72


def chunk_start(quarter):
    return jnp.where(
        quarter < 2,
        jnp.where(quarter == 0, CHUNK_STARTS[0], CHUNK_STARTS[1]),
        jnp.where(quarter == 2, CHUNK_STARTS[2], CHUNK_STARTS[3]),
    )


def assemble_kernel(spot, near, far, out, *, by_z):
    features = out.shape[-1]
    for other, pieces in enumerate((near, far)):

        @pl.when(pl.program_id(0) % 2 ^ spot[0] == other)
        def _(pieces=pieces):
            for order in range(4):
                start = pl.multiple_of(chunk_start(spot[1] ^ order), 8)
                for back in range(4):
                    z = (spot[2] + 4 - back) % 4
                    made = pieces[order, back, 0, :, :features]
                    if by_z:
                        out[z, 0, pl.ds(start, CHUNK), :] = made
                    else:
                        out[0, z, pl.ds(start, CHUNK), :] = made


def assemble(spot, pieces, rows, features, by_z=False):
    units = 2 * pieces[0].shape[2]
    part = pieces[0].shape[:2] + (1,) + pieces[0].shape[3:]
    if by_z:
        spec = pl.BlockSpec((4, 1, rows, features), lambda u, spot: (0, u, 0, 0))
        shape = (4, units, rows, features)
    else:
        spec = pl.BlockSpec((1, 4, rows, features), lambda u, spot: (u, 0, 0, 0))
        shape = (units, 4, rows, features)
    return call(
        functools.partial(assemble_kernel, by_z=by_z),
        (units,),
        [pl.BlockSpec(part, lambda u, spot: (0, 0, u // 2, 0, 0)) for p in pieces],
        spec,
        sds(shape, BF16),
        prefetch=1,
    )(spot, *pieces)


def finish_kernel(spot, *refs, units, across):
    groups = len(units)
    outs = refs[groups:]
    for pieces, group, outs_of in zip(refs[:groups], units, across):
        for unit, (target, place) in enumerate(zip(group, outs_of)):
            out = outs[target]
            features = pieces.shape[-1] if place is None else place[2]
            for order in range(4):
                start = pl.multiple_of(chunk_start(spot[1] ^ order), 8)
                made = pieces[spot[0] ^ (unit % 2), order, unit // 2, :, :features].astype(F32)
                row, column, _ = place
                out[pl.ds(row + start, CHUNK), column : column + features] = made


def finish(spot, groups, shapes, units, places):
    return call(
        functools.partial(finish_kernel, units=units, across=places),
        (1,),
        [pl.BlockSpec(g.shape, lambda u, spot, n=g.ndim: (0,) * n) for g in groups],
        [pl.BlockSpec(shape, lambda u, spot: (0, 0)) for shape in shapes],
        [sds(shape, F32) for shape in shapes],
        prefetch=1,
    )(spot, *groups)


def enter_kernel(x, gain, shift, weight, bias, first, mixed):
    width = mixed.shape[-1]
    features = first.shape[-1]

    @pl.when(pl.program_id(0) == 0)
    def _():
        normal, _ = normal_parts(x[:, : first.shape[-1]].astype(F32))
        first[...] = (normal * gain[...] + shift[...]).astype(BF16)

    made = dot(first[...], square(weight), NN) + bias[0]
    mixed[0, :, :features] = made.astype(BF16)
    mixed[0, :, features:] = jnp.zeros((x.shape[0], width - features), BF16)


def unit_spec(weights, pick):
    shape = (1,) + weights.shape[1:]
    return pl.BlockSpec(shape, lambda *at: (pick(*at), 0, 0, 0))


def enter(x, gain, shift, weights, bias):
    length, width = x.shape
    features = weights.shape[-1]
    return call(
        enter_kernel,
        (2,),
        [
            whole(x.shape),
            whole((1, features)),
            whole((1, features)),
            unit_spec(weights, lambda u: u),
            pl.BlockSpec((1, 1, features), lambda u: (u, 0, 0)),
        ],
        [whole((length, features)), pl.BlockSpec((1, length, width), lambda u: (u, 0, 0))],
        [sds((length, features), BF16), sds((2, length, width), BF16)],
    )(x, gain, shift, weights, bias)


def query_kernel(first, weight, bias, out):
    features = first.shape[-1]
    made = dot(first[...], square(weight), NN) + bias[...]
    out[:, :features] = made.astype(BF16)
    out[:, features:] = jnp.zeros((out.shape[0], out.shape[1] - features), BF16)


def query(first, weights, bias):
    length, features = first.shape
    width = -(-features // LANES) * LANES
    return call(
        query_kernel,
        (1,),
        [whole(first.shape), unit_spec(weights, lambda u: 0), whole((1, features))],
        whole((length, width)),
        sds((length, width), BF16),
    )(first, weights, bias)


def project_kernel(x, attended, weight, bias, gain, shift, hidden, second):
    features = hidden.shape[-1]
    branch = dot(attended[:, :features], square(weight), NN) + bias[...]
    stream = x[:, :features].astype(F32) + branch
    hidden[...] = stream
    normal, _ = normal_parts(stream)
    second[...] = (normal * gain[...] + shift[...]).astype(BF16)


def project(x, attended, weights, bias, gain, shift):
    length, features = x.shape[0], weights.shape[-1]
    row = whole((1, features))
    return call(
        project_kernel,
        (1,),
        [whole(x.shape), whole(attended.shape), unit_spec(weights, lambda u: 1), row, row, row],
        [whole((length, features)), whole((length, features))],
        [sds((length, features), F32), sds((length, features), BF16)],
    )(x, attended, weights, bias, gain, shift)


def feed_kernel(
    hidden, second, cot, up, down, up_bias, down_bias,
    result, up_grad, down_grad, up_bias_grad, second_grad, total,
):
    step = pl.program_id(0)
    features = hidden.shape[-1]
    cot = cot[:, :features]
    wide_up = square(up)
    wide_down = square(down)
    upward = dot(second[...], wide_up, NN) + up_bias[0]
    bell = 0.5 * (1.0 + lax.erf(upward * (0.5**0.5)))
    active = (upward * bell).astype(BF16)
    slope = bell + upward * jnp.exp(-0.5 * upward * upward) * ((0.5 / np.pi) ** 0.5)
    grad_up = (slope * dot(cot, wide_down, NT)).astype(BF16)
    out_part = dot(active, wide_down, NN)
    back_part = dot(grad_up, wide_up, NT)
    store_units(down_grad, dot(active, cot, TN))
    store_units(up_grad, dot(second[...], grad_up, TN))
    up_bias_grad[0] = jnp.sum(grad_up.astype(F32), 0, keepdims=True)

    @pl.when(step == 0)
    def _():
        total[...] = hidden[...] + down_bias[...] + out_part
        second_grad[...] = back_part

    @pl.when(step > 0)
    def _():
        total[...] += out_part
        second_grad[...] += back_part

    @pl.when(step == pl.num_programs(0) - 1)
    def _():
        result[:, :features] = total[...].astype(result.dtype)
        result[:, features:] = jnp.zeros((result.shape[0], result.shape[1] - features), result.dtype)


def feed(hidden, second, cot, up_weights, down_full, up_bias, down_bias):
    length, features = hidden.shape
    blocks, fsdp, rows, _ = up_weights.shape
    width = -(-features // LANES) * LANES
    row_spec = pl.BlockSpec((1, 1, features), lambda b: (b, 0, 0))
    down_spec = pl.BlockSpec((1, blocks, rows, features), lambda b: (b, 0, 0, 0))
    flat = whole(hidden.shape)
    return call(
        feed_kernel,
        (blocks,),
        [
            flat,
            flat,
            whole(cot.shape),
            unit_spec(up_weights, lambda b: b),
            down_spec,
            row_spec,
            whole((1, features)),
        ],
        [
            whole((length, width)),
            pl.BlockSpec((fsdp, 1, rows, width), lambda b: (0, b, 0, 0)),
            pl.BlockSpec((1, blocks, rows, width), lambda b: (b, 0, 0, 0)),
            row_spec,
            flat,
        ],
        [
            sds((length, width), BF16),
            sds((fsdp, blocks, rows, width), BF16),
            sds((fsdp, blocks, rows, width), BF16),
            sds((blocks, 1, features), F32),
            sds(hidden.shape, F32),
        ],
        [pltpu.VMEM(hidden.shape, F32)],
    )(hidden, second, cot, up_weights, down_full, up_bias, down_bias)


def store_units(target, made):
    features = made.shape[-1]
    lead = target.shape[:-1]
    target[..., :features] = made.astype(BF16).reshape(lead + (features,))
    target[..., features:] = jnp.zeros(lead + (target.shape[-1] - features,), BF16)


def turn_kernel(second_grad, hidden, cot, attended, weight, gain, stream_grad, att_grad, out_grad, sums):
    features = hidden.shape[-1]
    width = attended.shape[-1]
    normal, inverse = normal_parts(hidden[...])
    upstream = cot[:, :features].astype(F32)
    grad = second_grad[...]
    stream = upstream + normal_pull(normal, inverse, grad * gain[...])
    stream_grad[...] = stream
    low = stream.astype(BF16)
    made = dot(low, square(weight), NT)
    att_grad[:, :features] = made.astype(BF16)
    att_grad[:, features:] = jnp.zeros((hidden.shape[0], width - features), BF16)
    store_units(out_grad, dot(attended[:, :features], low, TN))
    sums[...] = jnp.concatenate(
        [
            jnp.sum(grad * normal, 0, keepdims=True),
            jnp.sum(grad, 0, keepdims=True),
            jnp.sum(low.astype(F32), 0, keepdims=True),
            jnp.sum(upstream, 0, keepdims=True),
            jnp.zeros((4, features), F32),
        ],
        0,
    )


def turn(second_grad, hidden, cot, attended, weights, gain):
    _, features = hidden.shape
    width = attended.shape[-1]
    unit = (weights.shape[1], weights.shape[2], width)
    flat = whole(hidden.shape)
    return call(
        turn_kernel,
        (1,),
        [flat, flat, whole(cot.shape), whole(attended.shape), unit_spec(weights, lambda u: 1), whole((1, features))],
        [flat, whole(attended.shape), whole(unit), whole((8, features))],
        [sds(hidden.shape, F32), sds(attended.shape, BF16), sds(unit, BF16), sds((8, features), F32)],
    )(second_grad, hidden, cot, attended, weights, gain)


def leave_query_kernel(query_grad, first, weight, back, unit_grad, column_sums):
    features = first.shape[-1]
    grad = query_grad[:, :features]
    back[...] = dot(grad, square(weight), NT)
    store_units(unit_grad, dot(first[...], grad, TN))
    column_sums[...] = jnp.sum(grad.astype(F32), 0, keepdims=True)


def leave_query(query_grad, first, weights):
    _, features = first.shape
    unit = (weights.shape[1], weights.shape[2], query_grad.shape[-1])
    return call(
        leave_query_kernel,
        (1,),
        [whole(query_grad.shape), whole(first.shape), unit_spec(weights, lambda u: 0)],
        [whole(first.shape), whole(unit), whole((1, features))],
        [sds(first.shape, F32), sds(unit, BF16), sds((1, features), F32)],
    )(query_grad, first, weights)


def leave_kernel(own, from_core, from_z, first, x, stream_grad, back, weight, gain, token_grad, unit_grad, column_sums, sums, total):
    step = pl.program_id(0)
    features = first.shape[-1]
    summed = own[0, :, :features] + from_core[0, :, :features].astype(F32) + from_z[0, :, :features].astype(F32)
    grad = summed.astype(BF16)
    part = dot(grad, square(weight), NT)
    store_units(unit_grad, dot(first[...], grad, TN))
    column_sums[0] = jnp.sum(grad.astype(F32), 0, keepdims=True)

    @pl.when(step == 0)
    def _():
        total[...] = back[...] + part

    @pl.when(step == 1)
    def _():
        normal, inverse = normal_parts(x[:, :features].astype(F32))
        grad_first = total[...] + part
        low = (stream_grad[...] + normal_pull(normal, inverse, grad_first * gain[...])).astype(BF16)
        token_grad[:, :features] = low
        token_grad[:, features:] = jnp.zeros((low.shape[0], token_grad.shape[1] - features), BF16)
        sums[...] = jnp.concatenate(
            [
                jnp.sum(grad_first * normal, 0, keepdims=True),
                jnp.sum(grad_first, 0, keepdims=True),
                jnp.zeros((6, features), F32),
            ],
            0,
        )


def leave(own, from_core, from_z, first, x, stream_grad, back, weights, gain):
    length, features = first.shape
    width = own.shape[-1]
    unit = (1, weights.shape[1], weights.shape[2], width)
    flat = whole(first.shape)
    kind = pl.BlockSpec((1, length, width), lambda u: (u, 0, 0))
    return call(
        leave_kernel,
        (2,),
        [kind, kind, kind, flat, whole(x.shape), flat, flat, unit_spec(weights, lambda u: u), whole((1, features))],
        [
            whole((length, width)),
            pl.BlockSpec(unit, lambda u: (u, 0, 0, 0)),
            pl.BlockSpec((1, 1, features), lambda u: (u, 0, 0)),
            whole((8, features)),
        ],
        [
            sds((length, width), BF16),
            sds((2,) + unit[1:], BF16),
            sds((2, 1, features), F32),
            sds((8, features), F32),
        ],
        [pltpu.VMEM(first.shape, F32)],
    )(own, from_core, from_z, first, x, stream_grad, back, weights, gain)


def block(
    tokens, w_qkv, qv_bias, w_out, out_bias, w_up, up_bias, w_down, down_bias,
    ln1_gain, ln1_bias, ln2_gain, ln2_bias, cotangent,
):
    _, length, features = tokens.shape
    rows = w_qkv.shape[0]
    half = length // 2
    width = -(-features // LANES) * LANES
    reps = lax.axis_size("rep")
    fsdp = lax.axis_size("fsdp")
    rep_at = lax.axis_index("rep")
    z_at = lax.axis_index("fsdp")
    core = rep_at % 2
    quarter = rep_at // 2 % 4
    grid = ("rep", "fsdp")

    def links(half):
        out = []
        for rep in range(reps):
            for z in range(fsdp):
                to, plane = destination(rep % 2, z, half)
                out.append((rep * fsdp + z, (rep - rep % 2 + to) * fsdp + plane))
        return out

    def flip(bits):
        return [(r * fsdp + z, (r ^ bits) * fsdp + z) for r in range(reps) for z in range(fsdp)]

    def shift(step):
        return [(r * fsdp + z, r * fsdp + (z + step) % fsdp) for r in range(reps) for z in range(fsdp)]

    def flip_z(bits):
        return [(r * fsdp + z, r * fsdp + (z ^ bits)) for r in range(reps) for z in range(fsdp)]

    def turned(perm):
        return [(b, a) for a, b in perm]

    move_a = links(0)
    move_b = links(1)
    to_core = flip(1)
    to_far = flip_z(1)

    def send(value, perm):
        return lax.ppermute(value, grid, perm)

    def swap(value):
        return jnp.concatenate([send(value[:half], move_a), send(value[half:], move_b)], 0)

    def swap_back(value):
        return jnp.concatenate(
            [send(value[:half], turned(move_a)), send(value[half:], turned(move_b))], 0
        )

    def take(value, at, axis=0):
        return lax.dynamic_index_in_dim(value, at, axis, keepdims=False)

    table = lax.dynamic_slice(
        jnp.asarray(task_table()), (core + 2 * (z_at // 2 ^ z_at % 2), 0), (1, 18)
    ).reshape(-1)
    spot = jnp.stack([core, quarter, z_at]).astype(jnp.int32)
    starts = jnp.asarray(CHUNK_STARTS, jnp.int32)

    def gather_group(piece):
        piece = jnp.pad(piece, ((0, 0), (0, 0), (0, width - features)))
        column = jnp.stack([piece] + [send(piece, shift(k)) for k in range(1, fsdp)])
        plane = jnp.stack([column] + [send(column, flip(2 * q)) for q in range(1, 4)])
        return plane, send(plane, to_core)

    def wide_sum(*parts):
        total = parts[0].astype(F32)
        for part in parts[1:]:
            total = total + part.astype(F32)
        return total.astype(BF16)

    def reduce_core(keep, give):
        return wide_sum(keep, send(give, to_core))

    x_at = quarter % 2
    y_at = quarter // 2

    def hold(values, after):
        return values if after is None else lax.optimization_barrier((values, after))[0]

    def stage_plane(total):
        inner = fsdp // 2

        def chunk(value, y, x):
            return lax.dynamic_slice_in_dim(value, starts[2 * y + x], CHUNK, 2)

        left, right = total[:inner], total[inner:]
        got = (
            send(jnp.stack([chunk(left, y, 1 - x_at) for y in range(2)]), flip(2)),
            send(jnp.stack([chunk(right, 1 - y_at, x) for x in range(2)]), flip(4)),
        )
        left = jnp.stack([chunk(left, y, x_at) for y in range(2)])
        right = jnp.stack([chunk(right, y_at, x) for x in range(2)])
        return left, right, got

    def stage_second(state, after=None):
        left, right, got = state
        left_got, right_got = hold(got, after)
        left, right = wide_sum(left, left_got), wide_sum(right, right_got)
        got = (send(take(left, 1 - y_at), flip(4)), send(take(right, 1 - x_at), flip(2)))
        return take(left, y_at), take(right, x_at), got

    def stage_line(state, after=None):
        left, right, got = state
        left_got, right_got = hold(got, after)
        mine = jnp.concatenate([wide_sum(left, left_got), wide_sum(right, right_got)], 0)
        got = tuple(send(take(mine, (z_at + k) % fsdp), shift(k)) for k in range(1, fsdp))
        return take(mine, z_at), got

    def stage_back(state, after=None):
        own, got = state
        own = wide_sum(own, *hold(got, after))
        bit = 8
        while bit < reps:
            own = wide_sum(own, send(own, flip(bit)))
            bit *= 2
        return own, tuple(send(own, flip(2 * q)) for q in range(1, 4))

    def stage_core(state, after=None):
        own, got = state
        four = jnp.stack([own, *hold(got, after)])
        return jnp.stack([four, send(four, to_core)])

    def reduce_small(value):
        value = value + send(value, to_core)
        for part in [send(value, flip(2 * q)) for q in range(1, 4)]:
            value = value + part
        got = [send(take(value, (z_at + k) % fsdp), shift(k)) for k in range(1, fsdp)]
        own = take(value, z_at)
        for part in got:
            own = own + part
        bit = 8
        while bit < reps:
            own = own + send(own, flip(bit))
            bit *= 2
        return own

    lane_pad = ((0, 0), (0, width - features))
    x = swap(jnp.pad(tokens[0], lane_pad))
    cot = swap(jnp.pad(cotangent[0], lane_pad))
    vectors = (qv_bias, out_bias, up_bias, down_bias, ln1_gain, ln1_bias, ln2_gain, ln2_bias)
    mine = jnp.concatenate(vectors)
    column = jnp.stack([mine] + [send(mine, shift(k)) for k in range(1, fsdp)])
    small = jnp.stack([take(column, (z_at - z) % fsdp) for z in range(fsdp)]).astype(F32)
    pieces = []
    start = 0
    for vector in vectors:
        pieces.append(small[:, start : start + vector.shape[0]].reshape(1, -1))
        start += vector.shape[0]
    qv_full, outb_full, upb_full, downb_full, gain_one, shift_one, gain_two, shift_two = pieces

    row_start = starts[quarter]
    kv_piece = lax.dynamic_slice(w_qkv, (row_start, (1 + core) * features), (CHUNK, features))
    query_piece = lax.dynamic_slice(w_qkv, (row_start, 0), (CHUNK, features))
    out_piece = lax.dynamic_slice(w_out, (row_start, 0), (CHUNK, features))
    kv_near, kv_far = gather_group(kv_piece[None])
    kv_weights = assemble(spot, (kv_near, kv_far), rows, features)
    qo_piece = jnp.where(core == 0, query_piece, out_piece)
    qo_weights = assemble(spot, gather_group(qo_piece[None]), rows, features)
    up_piece = jnp.stack(
        [
            lax.dynamic_slice(w_up, (row_start, (2 * g + core) * features), (CHUNK, features))
            for g in range(fsdp // 2)
        ]
    )
    up_weights = assemble(spot, gather_group(up_piece), rows, features)
    down_piece = jnp.stack(
        [
            lax.dynamic_slice(w_down, ((2 * g + core) * rows + row_start, 0), (CHUNK, features))
            for g in range(fsdp // 2)
        ]
    )
    down_full = assemble(spot, gather_group(down_piece), rows, features, by_z=True)

    kv_bias = jnp.stack([jnp.zeros((1, features), F32), qv_full[:, features:]])
    first, pair = enter(x, gain_one, shift_one, kv_weights, kv_bias)
    from_core = send(pair, to_core)
    from_far = send(pair, to_far)
    others = (from_core, from_far, send(from_far, to_core))
    queries = query(first, qo_weights, qv_full[:, :features])
    attended, lse = attention_forward(table, queries, pair, others)
    hidden, second = project(x, attended, qo_weights, outb_full, gain_two, shift_two)
    result, up_grad, down_grad, up_bias_grad, second_grad = feed(
        hidden, second, cot, up_weights, down_full, upb_full.reshape(-1, 1, features), downb_full
    )
    stream_grad, att_grad, out_grad, sums_two = turn(second_grad, hidden, cot, attended, qo_weights, gain_two)
    layer_out = swap_back(result)

    def split_pairs(grad):
        grad = grad.reshape((fsdp, fsdp // 2, 2) + grad.shape[2:])
        return take(grad, core, 2), take(grad, 1 - core, 2)

    up_sum = reduce_core(*split_pairs(up_grad))
    down_sum = reduce_core(*split_pairs(down_grad))
    up_state = stage_plane(up_sum)
    down_state = stage_plane(down_sum)
    dq, *rest = attention_backward(table, queries, pair, others, attended, att_grad, lse)
    own_pair, core_pair, far_pair, last_pair = rest
    far_sum = wide_sum(far_pair, send(last_pair, to_core))
    far_got = send(far_sum, to_far)
    core_got = send(core_pair, to_core)
    back, query_grad, query_sums = leave_query(dq, first, qo_weights)
    up_state = stage_second(up_state, far_sum)
    down_state = stage_second(down_state, far_sum)
    qo_sum = reduce_core(
        jnp.where(core == 0, query_grad, out_grad)[:, None],
        jnp.where(core == 0, out_grad, query_grad)[:, None],
    )
    qo_state = stage_plane(qo_sum)
    up_state = stage_line(up_state, query_grad)
    down_state = stage_line(down_state, query_grad)
    token_low, kv_grad, column_sums, sums_one = leave(
        own_pair, core_got, far_got, first, x, stream_grad, back, kv_weights, gain_one
    )
    kv_sum = reduce_core(take(kv_grad, core)[:, None], take(kv_grad, 1 - core)[:, None])
    qo_state = stage_second(qo_state, token_low)
    kv_state = stage_plane(kv_sum)
    kv_state = stage_second(kv_state)
    up_state = stage_back(up_state, kv_state[0])
    down_state = stage_back(down_state, kv_state[0])
    kv_state = stage_line(kv_state)
    line_done = kv_state[0]
    qo_state = stage_line(qo_state, line_done)
    kv_state = stage_back(kv_state)
    up_group = stage_core(up_state, kv_state[0])
    down_group = stage_core(down_state, kv_state[0])
    qo_state = stage_back(qo_state, kv_state[0])
    kv_group = stage_core(kv_state)
    qo_group = stage_core(qo_state)
    grad_tokens = hold(swap_back(token_low), line_done)[:, :features].astype(F32)
    layer_out = hold(layer_out, line_done)[:, :features].astype(F32)
    vectors = (
        sums_two[2], up_bias_grad, sums_two[3], sums_two[0], sums_two[1],
        jnp.concatenate([query_sums, column_sums[1]], 1), sums_one[0], sums_one[1],
    )
    own_row = reduce_small(jnp.concatenate([v.reshape(fsdp, -1) for v in vectors], 1))
    small_own = []
    start = 0
    for v in vectors:
        size = v.size // fsdp
        small_own.append(own_row[start : start + size])
        start += size
    out_b, up_b, down_b, gain_two_g, shift_two_g, qv_b, gain_one_g, shift_one_g = small_own
    beside = [(0, b * features, features) for b in range(fsdp)]
    below = [(b * rows, 0, features) for b in range(fsdp)]
    (up_own,) = finish(spot, [up_group], [(rows, fsdp * features)], [(0, 0, 0, 0)], [beside])
    (down_own,) = finish(spot, [down_group], [(features, features)], [(0, 0, 0, 0)], [below])
    qkv_own, out_own = finish(
        spot,
        [qo_group, kv_group],
        [(rows, 3 * features), (rows, features)],
        [(0, 1), (0, 0)],
        [[beside[0], beside[0]], beside[1:3]],
    )
    return (
        layer_out[None], grad_tokens[None],
        qkv_own, qv_b, out_own, out_b,
        up_own, up_b, down_own, down_b,
        gain_one_g, shift_one_g, gain_two_g, shift_two_g,
    )


def solution(mesh):
    data = P("rep", "fsdp", None)
    matrix = P("fsdp", None)
    vector = P("fsdp")
    return jax.shard_map(
        block,
        mesh=mesh,
        in_specs=(
            data, matrix, vector, matrix, vector, matrix, vector, matrix, vector,
            vector, vector, vector, vector, data,
        ),
        out_specs=(
            data, data, matrix, vector, matrix, vector, matrix, vector, matrix, vector,
            vector, vector, vector, vector,
        ),
        check_vma=False,
    )
```
